256 devices in a mesh: dp: 32 (over y, x, core), tensor: 8 (over z).
Axes of the slice: x: 4, y: 4, z: 8, core: 2. Of those that a mesh axis runs over, the one named last changes fastest.
Arguments:
- candidates: int32 [128, 16], P('dp'), may hold values from 0 to 63, all different within a row; in each aligned block of 4 rows (0 to 3, 4 to 7, ...) at most 2 rows name the same one
- sequence_place: int32 [64], replicated, may hold values from 0 to 63, each once
- activations: bfloat16 [64, 512, 28672], P('dp', None, 'tensor'), may hold values from -6 to 6
- gradients: bfloat16 [64, 512, 8192], P('dp', None, 'tensor'), may hold values from -6 to 6
- query_in: bfloat16 [128, 8, 28672], P('dp', None, 'tensor'), may hold values from -0.03125 to 0.03125
- query_out: bfloat16 [128, 8, 8192], P('dp', None, 'tensor'), may hold values from -0.0625 to 0.0625
Outputs:
- scores: float32 [128, 16, 512], P('dp', None, 'tensor')
The draws below stay inside these ranges and needn't reach their ends.
Inputs may be any that keep to these rules, and one draw needn't show every extreme that they name: `candidates`: each row names 16 different sequences; within the rows of one device (aligned blocks of 4 rows) no sequence is named more than 2 times. Each sequence id appears once; sequence s is stored at row sequence_place[s] of activations and gradients.
All inputs are finite; a program needn't handle non-finite values.
Results may differ from the reference program's by a relative error of at most 0.0003.
Values may be sent and summed in bfloat16 or wider, within the bound.
No kernel may reach another device: no remote copies, remote signals or barrier semaphores. Data moves between devices by JAX's collectives and lax.ppermute only.
A program may use at most 192 MiB of HBM per device.

```python
import math
import jax
import jax.numpy as jnp
import numpy as np
from jax import lax

D = 8192
FF = 28672
R = 8
CAND = 16
SEQ_LEN = 512
Q_DEV = 4
QUERIES = 128
NSEQ = 64
MOST = 2


def raised(array, rng, source, target, shards_of, factor):
    owner, partner = [(jnp.arange(array.shape[dim]) // (array.shape[dim] // shards_of)).reshape([-1 if axis == dim else 1 for axis in range(array.ndim)]) for dim in (source, target)]
    chosen = jax.random.permutation(rng, shards_of)[partner]
    strong = (owner == chosen) | (owner == (partner + shards_of // 2) % shards_of)
    return jnp.where(strong, factor * array, array)


def block_levels(stream_key, extent, shards, least, high):
    loudness = 1.0
    for axis_at, shards_of in shards:
        heights = jax.random.uniform(jax.random.fold_in(jax.random.fold_in(stream_key, 6), axis_at), (shards_of,), jnp.float32, least / len(shards), high / len(shards))
        loudness = loudness * jnp.repeat(jnp.exp(heights), extent[axis_at] // shards_of).reshape((-1,) + (1,) * (len(extent) - 1 - axis_at))
    return loudness


def deal_out(key, own, number, rows, number_of, top, limit, slope):
    order = jax.random.permutation(key, number_of)
    packed, ordinary = portions_of(number_of, rows * top, limit, slope, True), portions_of(number_of, rows * top, limit, slope, False)
    places = jnp.arange(number_of)

    def named(lengths, offset_by):
        used = int((lengths > 0).sum())
        fixed = max(1, used // 4)
        passed = fixed + (places - fixed + offset_by * (used - fixed)) % max(1, number_of - fixed)
        return jnp.zeros((number_of,), jnp.int32).at[order[jnp.where(places < fixed, places, passed)]].set(jnp.asarray(lengths, jnp.int32))

    lengths = jnp.where(number % 4 == 0, named(packed, number // 4), named(ordinary, number - number // 4 - 1))
    mixed = jax.random.permutation(jax.random.fold_in(own, 3), number_of)
    source_of, sink = mixed[0:number_of // 2 * 2:2], mixed[1:number_of // 2 * 2:2]
    room = jnp.minimum(lengths[source_of] - 1, limit - lengths[sink]) // 2
    room = jnp.where((source_of == order[0]) | (sink == order[0]) | (lengths[sink] == 0), 0, jnp.maximum(room, 0))
    passed = jax.random.randint(jax.random.fold_in(own, 4), (number_of // 2,), 0, 1 << 20) % (room + 1)
    lengths = lengths.at[source_of].add(-passed).at[sink].add(passed)
    items = jnp.searchsorted(jnp.cumsum(lengths), jnp.arange(rows * top), side="right").astype(jnp.int32)
    listing = items.reshape(top, rows).T
    listing = listing[jax.random.permutation(jax.random.fold_in(own, 1), rows)]
    offset_by = jax.random.randint(jax.random.fold_in(own, 2), (rows, 1), 0, top)
    return jnp.take_along_axis(listing, (jnp.arange(top)[None, :] + offset_by) % top, axis=1)


def portions_of(count, total, reach, slope, full):
    portions = [(1 << 20) // math.isqrt(rank ** slope) + 1 for rank in range(1, count + 1)]
    largest = reach if full else min(reach, max(-(-total // count), total * portions[0] // sum(portions)))
    least = 1 if total - largest >= count - 1 else 0
    holding, surplus = [largest] + [least] * (count - 1), total - largest - least * (count - 1)
    while surplus > 0:
        free = [i for i in range(1, count) if holding[i] < largest] or [i for i in range(1, count) if holding[i] < reach]
        mass, remaining = sum([portions[i] for i in free]), surplus
        for i in free:
            addition = min(reach - holding[i], max(1, remaining * portions[i] // mass), surplus)
            holding[i] = holding[i] + addition
            surplus = surplus - addition
    return np.array(holding)


def noise(own_key, shape, deviation, limit, pieces=(), kind=jnp.bfloat16):
    result = deviation * jax.random.normal(own_key, shape, jnp.float32)
    if pieces:
        result = result * block_levels(own_key, shape, pieces, -0.22, 0.18)
    return jnp.clip(result, -limit, limit).astype(kind)


def gaussian_with(key, extent, scale, limit, cuts, heavy, kind=jnp.bfloat16):
    drawn = scale * jax.random.normal(key, extent, jnp.float32)
    if cuts:
        drawn = drawn * block_levels(key, extent, cuts, -0.22, 0.18)
    return jnp.clip(raised(drawn, jax.random.fold_in(key, 3), *heavy), -limit, limit).astype(kind)


def setup_inputs(seed: int = 0) -> dict:
    arg_keys = jax.random.split(jax.random.key(seed), 7)
    candidates_keys = jax.random.split(jax.random.fold_in(arg_keys[0], 1), QUERIES // Q_DEV)
    candidates_turns = jax.random.permutation(jax.random.fold_in(arg_keys[0], 3), QUERIES // Q_DEV)
    candidates = jax.vmap(lambda own, number: deal_out(jax.random.fold_in(arg_keys[0], 2), own, number, Q_DEV, NSEQ, CAND, MOST, 2))(candidates_keys, candidates_turns).reshape((QUERIES, CAND))
    sequence_place = jax.random.permutation(arg_keys[1], NSEQ).astype(jnp.int32)
    activations = gaussian_with(arg_keys[2], (NSEQ, SEQ_LEN, FF), 1.0, 6.0, ((0, 32), (2, 8)), (2, 1, 8, 2.0))
    gradients = noise(arg_keys[3], (NSEQ, SEQ_LEN, D), 1.0, 6.0, ((0, 32), (2, 8)))
    query_in = noise(arg_keys[4], (QUERIES, R, FF), FF ** -0.5, 0.03125, ((0, 32), (2, 8)))
    query_out = noise(arg_keys[5], (QUERIES, R, D), D ** -0.5, 0.0625, ((0, 32), (2, 8)))
    return {"candidates": candidates, "sequence_place": sequence_place, "activations": activations, "gradients": gradients, "query_in": query_in, "query_out": query_out}


def reference(candidates, sequence_place, activations, gradients, query_in, query_out):
    target_rows = jnp.take(sequence_place, candidates, axis=0).astype(jnp.int32)

    def one_pair(pair_index):
        query = pair_index // CAND
        column = pair_index % CAND
        target = target_rows[query, column]
        token_acts = lax.dynamic_index_in_dim(activations, target, 0, keepdims=False)
        token_grads = lax.dynamic_index_in_dim(gradients, target, 0, keepdims=False)
        factor_in = lax.dynamic_index_in_dim(query_in, query, 0, keepdims=False)
        factor_out = lax.dynamic_index_in_dim(query_out, query, 0, keepdims=False)
        input_side = jnp.dot(factor_in, token_acts.T, preferred_element_type=jnp.float32)
        output_side = jnp.dot(factor_out, token_grads.T, preferred_element_type=jnp.float32)
        return jnp.sum(input_side * output_side, axis=0)

    flat_scores = lax.map(one_pair, jnp.arange(QUERIES * CAND, dtype=jnp.int32))
    return flat_scores.reshape(QUERIES, CAND, SEQ_LEN)
```

```python
import functools

import jax
import jax.numpy as jnp
from jax import lax
from jax.experimental import pallas as pl
from jax.experimental.pallas import tpu as pltpu
from jax.sharding import PartitionSpec as P

SIDE = 4


def place(y, x, core):
    return ((y % SIDE) * SIDE + x % SIDE) * 2 + core


def hop(phase, sign):
    pairs = []
    for y in range(SIDE):
        for x in range(SIDE):
            for core in range(2):
                along_x = (phase == 1) == (core == 0)
                dy, dx = (0, sign) if along_x else (sign, 0)
                pairs.append((place(y, x, core), place(y + dy, x + dx, core)))
    return pairs


PARTNER = [(i, i ^ 1) for i in range(2 * SIDE * SIDE)]
SAME_CORE = [[2 * chip + core for chip in range(SIDE * SIDE)] for core in range(2)]
OFFSETS = (0, -1, 1, 2)


def project_kernel(slots, in_width, out_width, pick, *refs):
    groups = refs[:4]
    acts, grads, part, rows, act_buf, grad_buf, row_sem, act_sem, grad_sem = refs[4:]
    seqs = acts.shape[0]
    sources = slots // 2

    def fetch(j, slot):
        for m in range(2):
            for n in range(sources):
                query = pick[(j * 2 + m) * sources + n]
                src = groups[n // 4].at[n % 4, query]
                pltpu.make_async_copy(
                    src, rows.at[slot, m * sources + n], row_sem.at[slot]
                ).start()
        pltpu.make_async_copy(acts.at[j], act_buf.at[slot], act_sem.at[slot]).start()
        pltpu.make_async_copy(grads.at[j], grad_buf.at[slot], grad_sem.at[slot]).start()

    def arrive(j, slot):
        pltpu.make_async_copy(rows.at[slot], rows.at[slot], row_sem.at[slot]).wait()
        pltpu.make_async_copy(acts.at[j], act_buf.at[slot], act_sem.at[slot]).wait()
        pltpu.make_async_copy(grads.at[j], grad_buf.at[slot], grad_sem.at[slot]).wait()

    for j in range(seqs):
        fetch(j, j)
    contract = (((1,), (1,)), ((), ()))
    width = slots * 8
    for j in range(seqs):
        arrive(j, j)
        chosen = rows[j].reshape(width, rows.shape[-1])
        side_in = lax.dot_general(
            act_buf[j], chosen[:, :in_width], contract, preferred_element_type=jnp.float32
        )
        side_out = lax.dot_general(
            grad_buf[j],
            chosen[:, in_width : in_width + out_width],
            contract,
            preferred_element_type=jnp.float32,
        )
        shares = part.shape[0]
        part[:, j, :, :width] = side_in.reshape(shares, -1, width)
        part[:, j, :, width:] = side_out.reshape(shares, -1, width)


def project(pick, groups, acts, grads, shares):
    sources = 16
    slots = 2 * sources
    seqs, tokens, in_width = acts.shape
    out_width = grads.shape[-1]
    row_width = groups[0].shape[-1]
    return pl.pallas_call(
        functools.partial(project_kernel, slots, in_width, out_width),
        grid_spec=pltpu.PrefetchScalarGridSpec(
            num_scalar_prefetch=1,
            grid=(1,),
            in_specs=[pl.BlockSpec(memory_space=pl.ANY)] * 6,
            out_specs=pl.BlockSpec(
                (shares, seqs, tokens // shares, slots * 16), lambda i, pick: (0, 0, 0, 0)
            ),
            scratch_shapes=[
                pltpu.VMEM((seqs, slots, 8, row_width), jnp.bfloat16),
                pltpu.VMEM((seqs, tokens, in_width), jnp.bfloat16),
                pltpu.VMEM((seqs, tokens, out_width), jnp.bfloat16),
                pltpu.SemaphoreType.DMA((seqs,)),
                pltpu.SemaphoreType.DMA((seqs,)),
                pltpu.SemaphoreType.DMA((seqs,)),
            ],
        ),
        out_shape=jax.ShapeDtypeStruct(
            (shares, seqs, tokens // shares, slots * 16), jnp.float32
        ),
        cost_estimate=pl.CostEstimate(
            flops=2 * seqs * tokens * slots * 8 * (in_width + out_width),
            bytes_accessed=seqs * (tokens + slots * 8) * (in_width + out_width) * 2,
            transcendentals=0,
        ),
        compiler_params=pltpu.CompilerParams(vmem_limit_bytes=48 * 1024 * 1024),
        name="project",
    )(pick, *groups, acts, grads)


def score_kernel(info, *refs):
    out = refs[-1]
    sources = out.shape[0]
    for half in range(2):
        own, left, right = refs[3 * half : 3 * half + 3]
        for j in range(2):
            total = own[0, j] + left[j] + right[j]
            width = total.shape[-1] // 2
            product = total[:, :width] * total[:, width:]
            ranked = product.T.reshape(2 * sources, 8, product.shape[0])
            summed = jnp.sum(ranked, axis=1)
            line = jnp.concatenate([summed[:sources], summed[sources:]], axis=1)
            for n in range(sources):
                out[info[1 + n], 2 * half + j, :] = line[n]


def score(info, terms, shares):
    own_a, left_a, right_a, own_b, left_b, right_b = terms
    _, seqs, tokens, width = own_a.shape
    own_spec = pl.BlockSpec((1, seqs, tokens, width), lambda i, info: (info[0], 0, 0, 0))
    term_spec = pl.BlockSpec((seqs, tokens, width), lambda i, info: (0, 0, 0))
    return pl.pallas_call(
        score_kernel,
        grid_spec=pltpu.PrefetchScalarGridSpec(
            num_scalar_prefetch=1,
            grid=(1,),
            in_specs=[own_spec, term_spec, term_spec] * 2,
            out_specs=pl.BlockSpec((16, 2 * seqs, 2 * tokens), lambda i, info: (0, 0, 0)),
        ),
        out_shape=jax.ShapeDtypeStruct((16, 2 * seqs, 2 * tokens), jnp.float32),
        name="score",
    )(info, *terms)


def choose_kernel(where, returned, out):
    queries, count, tokens = out.shape
    for q in range(queries):
        for c in range(count):
            at = where[q * count + c]
            line = returned[at // 2]
            slot = at % 2
            line = jnp.where(slot == 0, line[:tokens], line[tokens:])
            out[q, c, :] = line


def choose(where, returned, queries, count):
    lines, width = returned.shape
    return pl.pallas_call(
        choose_kernel,
        grid_spec=pltpu.PrefetchScalarGridSpec(
            num_scalar_prefetch=1,
            grid=(1,),
            in_specs=[pl.BlockSpec((lines, width), lambda i, where: (0, 0))],
            out_specs=pl.BlockSpec((queries, count, width // 2), lambda i, where: (0, 0, 0)),
        ),
        out_shape=jax.ShapeDtypeStruct((queries, count, width // 2), jnp.float32),
        name="choose",
    )(where, returned)


def local(candidates, sequence_place, activations, gradients, query_in, query_out):
    queries, count = candidates.shape
    total = sequence_place.shape[0]
    shares = lax.axis_size("tensor")
    device = lax.axis_index("dp")
    z = lax.axis_index("tensor")
    core = device % 2
    chip = device // 2
    in_width = query_in.shape[-1]
    out_width = query_out.shape[-1]

    other_acts = lax.ppermute(activations, "dp", PARTNER)
    other_grads = lax.ppermute(gradients, "dp", PARTNER)

    target_rows = jnp.take(sequence_place, candidates, axis=0)
    positions = jnp.arange(total, dtype=jnp.int32)
    listed = jnp.any(target_rows[:, :, None] == positions, axis=1)
    number = jnp.arange(queries, dtype=jnp.int32)[:, None]
    flags = listed.astype(jnp.int32)
    before = jnp.sum(
        jnp.where(number[:, :, None] > number[None, :, 0:1].reshape(1, queries, 1), flags[None], 0),
        axis=1,
    )
    slot_query = jnp.stack(
        [jnp.sum(jnp.where(listed & (before == m), number, 0), axis=0) for m in range(2)]
    )
    table = slot_query.reshape(1, 1, 2 * total).astype(jnp.bfloat16)
    block = jnp.concatenate(
        [query_in, query_out, jnp.broadcast_to(table, (queries, 8, 2 * total))], axis=-1
    )

    dp = lambda array, phase, sign: lax.ppermute(array, "dp", hop(phase, sign))
    below = dp(block, 1, 1)
    above = dp(block, 1, -1)
    half = queries // 2
    far = jnp.concatenate([dp(below[:half], 1, 1), dp(above[half:], 1, -1)])
    line = jnp.stack([block, below, above, far])
    line_below = dp(line, 2, 1)
    line_above = dp(line, 2, -1)
    line_far = jnp.concatenate([dp(line_below[:2], 2, 1), dp(line_above[2:], 2, -1)])
    groups = (line, line_below, line_above, line_far)

    tables = jnp.concatenate([g[:, 0, 0, in_width + out_width :] for g in groups])
    tables = tables.reshape(16, 2, total)

    def picks(owner):
        chosen = lax.dynamic_slice_in_dim(tables, 2 * owner, 2, 2)
        return chosen.transpose(2, 1, 0).reshape(-1).astype(jnp.int32)

    part_a = project(picks(device), groups, activations, gradients, shares)
    part_b = project(picks(device ^ 1), groups, other_acts, other_grads, shares)

    ring = {1: [(i, (i + 1) % shares) for i in range(shares)]}
    ring[-1] = [(i, (i - 1) % shares) for i in range(shares)]

    def share(part, offset):
        return lax.dynamic_index_in_dim(part, (z + offset) % shares, 0, keepdims=False)

    def send(array, sign):
        return lax.ppermute(array, "tensor", ring[sign])

    far_a, far_b = shares // 2, shares - 1 - shares // 2
    moving = {}
    for step in range(far_a):
        for name, part, plus, minus in (("a", part_a, far_a, far_b), ("b", part_b, far_b, far_a)):
            for sign, length in ((1, plus), (-1, minus)):
                if step >= length:
                    continue
                mine = share(part, sign * (length - step))
                if step:
                    mine = mine + moving[name, sign]
                moving[name, sign] = send(mine, sign)

    offsets = jnp.array(OFFSETS, jnp.int32)
    y, x = chip // SIDE, chip % SIDE
    second, first = offsets[:, None], offsets[None, :]
    row = jnp.where(core == 0, (y + second) % SIDE, (y + first) % SIDE)
    col = jnp.where(core == 0, (x + first) % SIDE, (x + second) % SIDE)
    order = (row * SIDE + col).reshape(-1)
    info = jnp.concatenate([z[None], order]).astype(jnp.int32)
    terms = []
    for name, part in (("a", part_a), ("b", part_b)):
        terms += [part, moving[name, 1], moving[name, -1]]
    scores = score(info, terms, shares)
    returned = lax.all_to_all(
        scores, "dp", split_axis=0, concat_axis=0, tiled=True, axis_index_groups=SAME_CORE
    )

    slot = jnp.sum(jnp.where(target_rows[:, :, None] == positions, before[:, None, :], 0), axis=2)
    kind = jnp.where((target_rows // 2) % 2 == core, 0, 2) + target_rows % 2
    where = ((target_rows // 4) * 4 + kind) * 2 + slot
    return choose(where.reshape(-1), returned.reshape(64, -1), queries, count)


def solution(mesh):
    return jax.shard_map(
        local,
        mesh=mesh,
        in_specs=(
            P("dp", None),
            P(),
            P("dp", None, "tensor"),
            P("dp", None, "tensor"),
            P("dp", None, "tensor"),
            P("dp", None, "tensor"),
        ),
        out_specs=P("dp", None, "tensor"),
        check_vma=False,
    )
```

```python
import functools

import jax
import jax.numpy as jnp
from jax import lax
from jax.experimental import pallas as pl
from jax.experimental.pallas import tpu as pltpu
from jax.sharding import PartitionSpec as P


SIDE = 4


def place(y, x, core):
    return ((y % SIDE) * SIDE + x % SIDE) * 2 + core


def hop(phase, distance):
    pairs = []
    for y in range(SIDE):
        for x in range(SIDE):
            for core in range(2):
                along_x = (phase == 1) == (core == 0)
                dy, dx = (0, distance) if along_x else (distance, 0)
                pairs.append((place(y, x, core), place(y + dy, x + dx, core)))
    return pairs


PARTNER = [(i, i ^ 1) for i in range(2 * SIDE * SIDE)]
SAME_CORE = [[2 * chip + core for chip in range(SIDE * SIDE)] for core in range(2)]
OFFSETS = tuple((second, first) for first in (0, -1, 1, 2) for second in (0, -1, 1, 2))
HEAD = 19
MIB = 1024 * 1024
VMEM = pl.BlockSpec(memory_space=pltpu.VMEM)
SMEM = pl.BlockSpec(memory_space=pltpu.SMEM)
HBM = pl.BlockSpec(memory_space=pltpu.HBM)


def on_chip(arrays):
    return [pltpu.with_memory_space_constraint(a, pltpu.VMEM) for a in arrays]


def hold_kernel(info, *refs):
    count = len(refs) // 2
    sems = refs[-1]
    copies = [
        pltpu.make_async_copy(refs[i], refs[count + i], sems.at[i]) for i in range(count)
    ]
    for copy in copies:
        copy.start()
    for copy in copies:
        copy.wait()


def hold(info, *arrays):
    return pl.pallas_call(
        hold_kernel,
        in_specs=[SMEM] + [HBM] * len(arrays),
        out_specs=[VMEM] * len(arrays),
        out_shape=[jax.ShapeDtypeStruct(a.shape, a.dtype) for a in arrays],
        scratch_shapes=[pltpu.SemaphoreType.DMA((len(arrays),))],
        cost_estimate=pl.CostEstimate(
            flops=0, bytes_accessed=4 * sum(a.size for a in arrays), transcendentals=0
        ),
        compiler_params=pltpu.CompilerParams(vmem_limit_bytes=2 * MIB),
        name="hold",
    )(info, *[pltpu.with_memory_space_constraint(a, pltpu.HBM) for a in arrays])


def project_kernel(lengths, first, info, *refs):
    blocks, (acts, grads, part, own, plus, minus) = refs[:16], refs[16:22]
    table, table_scalars, sem, rows = refs[22], refs[23], refs[24], refs[25:27]
    in_width, out_width = acts.shape[-1], grads.shape[-1]
    shares, seqs = part.shape[0], part.shape[1]
    sources = table.shape[0]
    width = 16 * sources
    z, base = info[0], info[first]
    for n in range(sources):
        entry = blocks[n][0, :, in_width + out_width :].astype(jnp.float32)
        table[n : n + 1, :] = entry[0:1].astype(jnp.int32)
    copy = pltpu.make_async_copy(table, table_scalars, sem)
    copy.start()
    copy.wait()
    contract = (((1,), (1,)), ((), ()))
    for j in range(seqs):
        for m in range(2):
            for n in range(sources):
                query = table_scalars[n, m * 64 + base + j]
                rows[j][m * sources + n] = blocks[n][query]
    for j in range(seqs):
        chosen = rows[j][...].reshape(width, rows[j].shape[-1])
        side_in = lax.dot_general(
            acts[j], chosen[:, :in_width], contract, preferred_element_type=jnp.float32
        )
        side_out = lax.dot_general(
            grads[j],
            chosen[:, in_width : in_width + out_width],
            contract,
            preferred_element_type=jnp.float32,
        )
        part[:, j, :, :width] = side_in.reshape(shares, -1, width)
        part[:, j, :, width:] = side_out.reshape(shares, -1, width)
    own[...] = part[z]
    plus[...] = part[lax.rem(z + lengths[0], shares)]
    minus[...] = part[lax.rem(z + shares - lengths[1], shares)]


def project(info, first, blocks, acts, grads, shares, lengths):
    sources = 16
    seqs, tokens, in_width = acts.shape
    out_width = grads.shape[-1]
    row_width = blocks[0].shape[-1]
    share = (seqs, tokens // shares, sources * 32)
    return pl.pallas_call(
        functools.partial(project_kernel, lengths, first),
        in_specs=[SMEM] + [VMEM] * 18,
        out_specs=[VMEM] * 4,
        scratch_shapes=[
            pltpu.VMEM((sources, 128), jnp.int32),
            pltpu.SMEM((sources, 128), jnp.int32),
            pltpu.SemaphoreType.DMA,
        ]
        + [pltpu.VMEM((2 * sources, 8, row_width), jnp.bfloat16)] * 2,
        out_shape=[jax.ShapeDtypeStruct((shares, *share), jnp.float32)]
        + [jax.ShapeDtypeStruct(share, jnp.float32)] * 3,
        cost_estimate=pl.CostEstimate(
            flops=2 * seqs * tokens * sources * 16 * (in_width + out_width),
            bytes_accessed=seqs * (tokens + sources * 16) * (in_width + out_width) * 2,
            transcendentals=0,
        ),
        compiler_params=pltpu.CompilerParams(vmem_limit_bytes=18 * MIB),
        name="project",
    )(info, *on_chip((*blocks, acts, grads)))


def add_kernel(offsets, info, part, *refs):
    shares = part.shape[0]
    count = len(offsets)
    for offset, came, out in zip(offsets, refs[:count], refs[count:]):
        out[...] = came[...] + part[lax.rem(info[0] + offset + shares, shares)]


def add_shares(info, part, came, offsets):
    return pl.pallas_call(
        functools.partial(add_kernel, tuple(offsets)),
        in_specs=[SMEM] + [VMEM] * (1 + len(came)),
        out_specs=[VMEM] * len(came),
        out_shape=[jax.ShapeDtypeStruct(a.shape, a.dtype) for a in came],
        cost_estimate=pl.CostEstimate(
            flops=came[0].size * len(came), bytes_accessed=12 * came[0].size, transcendentals=0
        ),
        compiler_params=pltpu.CompilerParams(vmem_limit_bytes=2 * MIB),
        name="add_shares",
    )(info, *on_chip((part, *came)))


def score_kernel(info, *refs):
    out = refs[-1]
    for half in range(2):
        own, left, right = refs[3 * half : 3 * half + 3]
        for j in range(left.shape[0]):
            total = own[j] + left[j] + right[j]
            width = total.shape[-1] // 2
            product = total[:, :width] * total[:, width:]
            sources = width // 16
            ranked = product.T.reshape(2 * sources, 8, product.shape[0])
            summed = jnp.sum(ranked, axis=1)
            line = jnp.concatenate([summed[:sources], summed[sources:]], axis=1)
            for n in range(sources):
                out[info[3 + n], 2 * half + j, :] = line[n]


def score(info, terms):
    seqs, tokens, _ = terms[0].shape
    return pl.pallas_call(
        score_kernel,
        in_specs=[SMEM] + [VMEM] * 6,
        out_specs=VMEM,
        out_shape=jax.ShapeDtypeStruct((16, 2 * seqs, 2 * tokens), jnp.float32),
        compiler_params=pltpu.CompilerParams(vmem_limit_bytes=4 * MIB),
        name="score",
    )(info, *on_chip(terms))


def choose_kernel(where, returned, out):
    queries, count, tokens = out.shape
    for q in range(queries):
        for c in range(count):
            at = where[HEAD + q * count + c]
            line = returned[at // 2]
            slot = at % 2
            line = jnp.where(slot == 0, line[:tokens], line[tokens:])
            out[q, c, :] = line


def choose(where, returned, queries, count):
    _, width = returned.shape
    return pl.pallas_call(
        choose_kernel,
        in_specs=[SMEM, VMEM],
        out_specs=VMEM,
        out_shape=jax.ShapeDtypeStruct((queries, count, width // 2), jnp.float32),
        compiler_params=pltpu.CompilerParams(vmem_limit_bytes=4 * MIB),
        name="choose",
    )(where, *on_chip([returned]))


def local(candidates, sequence_place, activations, gradients, query_in, query_out):
    queries, count = candidates.shape
    total = sequence_place.shape[0]
    shares = lax.axis_size("tensor")
    device = lax.axis_index("dp")
    z = lax.axis_index("tensor")
    core = device % 2
    chip = device // 2

    other_acts = lax.ppermute(activations, "dp", PARTNER)
    other_grads = lax.ppermute(gradients, "dp", PARTNER)

    target_rows = jnp.take(sequence_place, candidates, axis=0)
    positions = jnp.arange(total, dtype=jnp.int32)
    listed = jnp.any(target_rows[:, :, None] == positions, axis=1)
    number = jnp.arange(queries, dtype=jnp.int32)[:, None]
    flags = listed.astype(jnp.int32)
    before = jnp.sum(
        jnp.where(number[:, :, None] > number[None, :, 0:1].reshape(1, queries, 1), flags[None], 0),
        axis=1,
    )
    slot_query = jnp.stack(
        [jnp.sum(jnp.where(listed & (before == m), number, 0), axis=0) for m in range(2)]
    )
    table = slot_query.reshape(1, 1, 2 * total).astype(jnp.bfloat16)
    block = jnp.concatenate(
        [query_in, query_out, jnp.broadcast_to(table, (queries, 8, 2 * total))], axis=-1
    )

    def dp(array, phase, distance):
        return lax.ppermute(array, "dp", hop(phase, distance))

    blocks = []
    lines = [("block", block), ("below", dp(block, 1, 1))]
    lines += [("above", dp(block, 1, -1)), ("far", dp(block, 1, 2))]
    for name, array in lines:
        up, down = dp(array, 2, 1), dp(array, 2, -1)
        on = dp(up, 2, 1) if name == "below" else dp(down, 2, -1)
        blocks += [array, up, down, on]

    offsets = jnp.array(OFFSETS, jnp.int32)
    y, x = chip // SIDE, chip % SIDE
    second_axis, first_axis = offsets[:, 0], offsets[:, 1]
    row = (y + jnp.where(core == 0, second_axis, first_axis)) % SIDE
    col = (x + jnp.where(core == 0, first_axis, second_axis)) % SIDE
    slot = jnp.sum(jnp.where(target_rows[:, :, None] == positions, before[:, None, :], 0), axis=2)
    kind = jnp.where((target_rows // 2) % 2 == core, 0, 2) + target_rows % 2
    where = ((target_rows // 4) * 4 + kind) * 2 + slot
    heads = jnp.stack([z, 2 * device, 2 * (device ^ 1)])
    info = jnp.concatenate([heads, row * SIDE + col, where.reshape(-1)]).astype(jnp.int32)

    ring = {1: [(i, (i + 1) % shares) for i in range(shares)]}
    ring[-1] = [(i, (i - 1) % shares) for i in range(shares)]

    def send(array, sign):
        return lax.ppermute(array, "tensor", ring[sign])

    held_a = hold(info, activations, gradients)
    held_b = (*hold(info, other_acts), other_grads)
    far_a, far_b = shares // 2, shares - 1 - shares // 2
    streams = []
    for base, held, lengths in ((1, held_a, (far_a, far_b)), (2, held_b, (far_b, far_a))):
        part, own, plus, minus = project(info, base, blocks, *held, shares, lengths)
        streams.append([own, send(plus, 1), send(minus, -1), part, lengths])
    for step in range(1, far_a):
        for stream in streams:
            _, plus, minus, part, lengths = stream
            came, signs = [], []
            for sign, array, length in ((1, plus, lengths[0]), (-1, minus, lengths[1])):
                if step < length:
                    came.append(array)
                    signs.append(sign)
            away = [s * (lengths[0 if s > 0 else 1] - step) for s in signs]
            sums = add_shares(info, part, came, away)
            for sign, total_so_far in zip(signs, sums):
                stream[1 if sign > 0 else 2] = send(total_so_far, sign)

    scores = score(info, [a for stream in streams for a in stream[:3]])
    returned = lax.all_to_all(
        scores, "dp", split_axis=0, concat_axis=0, tiled=True, axis_index_groups=SAME_CORE
    )

    return choose(info, returned.reshape(64, -1), queries, count)


def solution(mesh):
    return jax.shard_map(
        local,
        mesh=mesh,
        in_specs=(
            P("dp", None),
            P(),
            P("dp", None, "tensor"),
            P("dp", None, "tensor"),
            P("dp", None, "tensor"),
            P("dp", None, "tensor"),
        ),
        out_specs=P("dp", None, "tensor"),
        check_vma=False,
    )
```

```python
import functools

import jax
import jax.numpy as jnp
from jax import lax
from jax.experimental import pallas as pl
from jax.experimental.pallas import tpu as pltpu
from jax.sharding import PartitionSpec as P


SIDE = 4


def place(y, x, core):
    return ((y % SIDE) * SIDE + x % SIDE) * 2 + core


def hop(phase, distance):
    pairs = []
    for y in range(SIDE):
        for x in range(SIDE):
            for core in range(2):
                along_x = (phase == 1) == (core == 0)
                dy, dx = (0, distance) if along_x else (distance, 0)
                pairs.append((place(y, x, core), place(y + dy, x + dx, core)))
    return pairs


PARTNER = [(i, i ^ 1) for i in range(2 * SIDE * SIDE)]
SAME_CORE = [[2 * chip + core for chip in range(SIDE * SIDE)] for core in range(2)]
OFFSETS = tuple((second, first) for first in (0, -1, 1, 2) for second in (0, -1, 1, 2))
HEAD = 19
MIB = 1024 * 1024
VMEM = pl.BlockSpec(memory_space=pltpu.VMEM)
SMEM = pl.BlockSpec(memory_space=pltpu.SMEM)
HBM = pl.BlockSpec(memory_space=pltpu.HBM)


def on_chip(arrays):
    return [pltpu.with_memory_space_constraint(a, pltpu.VMEM) for a in arrays]


def hold_kernel(places, info, *refs):
    count = len(places)
    sems = refs[-1]
    copies = [
        pltpu.make_async_copy(
            refs[i] if at is None else refs[i].at[at], refs[count + i], sems.at[i]
        )
        for i, at in enumerate(places)
    ]
    for copy in copies:
        copy.start()
    for copy in copies:
        copy.wait()


def hold(info, *arrays):
    places = tuple(at for _, at in arrays)
    outs = [
        jax.ShapeDtypeStruct(a.shape if at is None else a.shape[1:], a.dtype) for a, at in arrays
    ]
    return pl.pallas_call(
        functools.partial(hold_kernel, places),
        in_specs=[SMEM] + [HBM] * len(arrays),
        out_specs=[VMEM] * len(arrays),
        out_shape=outs,
        scratch_shapes=[pltpu.SemaphoreType.DMA((len(arrays),))],
        cost_estimate=pl.CostEstimate(
            flops=0, bytes_accessed=4 * sum(a.size for a in outs), transcendentals=0
        ),
        compiler_params=pltpu.CompilerParams(vmem_limit_bytes=2 * MIB),
        name="hold",
    )(info, *[pltpu.with_memory_space_constraint(a, pltpu.HBM) for a, _ in arrays])


def project_kernel(lengths, first, info, *refs):
    blocks, acts, (grads, part, own, plus, minus) = refs[:16], refs[16:18], refs[18:23]
    table, table_scalars, sem, rows = refs[23], refs[24], refs[25], refs[26:28]
    in_width, out_width = acts[0].shape[-1], grads.shape[-1]
    shares, seqs = part.shape[0], part.shape[1]
    sources = table.shape[0]
    width = 16 * sources
    z, base = info[0], info[first]
    for n in range(sources):
        entry = blocks[n][0, :, in_width + out_width :].astype(jnp.float32)
        table[n : n + 1, :] = entry[0:1].astype(jnp.int32)
    copy = pltpu.make_async_copy(table, table_scalars, sem)
    copy.start()
    copy.wait()
    contract = (((1,), (1,)), ((), ()))
    for j in range(seqs):
        for m in range(2):
            for n in range(sources):
                query = table_scalars[n, m * 64 + base + j]
                rows[j][m * sources + n] = blocks[n][query]
    for j in range(seqs):
        chosen = rows[j][...].reshape(width, rows[j].shape[-1])
        side_in = lax.dot_general(
            acts[j][...], chosen[:, :in_width], contract, preferred_element_type=jnp.float32
        )
        side_out = lax.dot_general(
            grads[j],
            chosen[:, in_width : in_width + out_width],
            contract,
            preferred_element_type=jnp.float32,
        )
        part[:, j, :, :width] = side_in.reshape(shares, -1, width)
        part[:, j, :, width:] = side_out.reshape(shares, -1, width)
    own[...] = part[z]
    plus[...] = part[lax.rem(z + lengths[0], shares)]
    minus[...] = part[lax.rem(z + shares - lengths[1], shares)]


def project(info, first, blocks, acts, grads, shares, lengths):
    sources = 16
    seqs, (tokens, in_width) = len(acts), acts[0].shape
    out_width = grads.shape[-1]
    row_width = blocks[0].shape[-1]
    share = (seqs, tokens // shares, sources * 32)
    return pl.pallas_call(
        functools.partial(project_kernel, lengths, first),
        in_specs=[SMEM] + [VMEM] * 19,
        out_specs=[VMEM] * 4,
        scratch_shapes=[
            pltpu.VMEM((sources, 128), jnp.int32),
            pltpu.SMEM((sources, 128), jnp.int32),
            pltpu.SemaphoreType.DMA,
        ]
        + [pltpu.VMEM((2 * sources, 8, row_width), jnp.bfloat16)] * 2,
        out_shape=[jax.ShapeDtypeStruct((shares, *share), jnp.float32)]
        + [jax.ShapeDtypeStruct(share, jnp.float32)] * 3,
        cost_estimate=pl.CostEstimate(
            flops=2 * seqs * tokens * sources * 16 * (in_width + out_width),
            bytes_accessed=seqs * (tokens + sources * 16) * (in_width + out_width) * 2,
            transcendentals=0,
        ),
        compiler_params=pltpu.CompilerParams(vmem_limit_bytes=18 * MIB),
        name="project",
    )(info, *on_chip((*blocks, *acts, grads)))


def add_kernel(offsets, info, part, *refs):
    shares = part.shape[0]
    count = len(offsets)
    for offset, came, out in zip(offsets, refs[:count], refs[count:]):
        out[...] = came[...] + part[lax.rem(info[0] + offset + shares, shares)]


def add_shares(info, part, came, offsets):
    return pl.pallas_call(
        functools.partial(add_kernel, tuple(offsets)),
        in_specs=[SMEM] + [VMEM] * (1 + len(came)),
        out_specs=[VMEM] * len(came),
        out_shape=[jax.ShapeDtypeStruct(a.shape, a.dtype) for a in came],
        cost_estimate=pl.CostEstimate(
            flops=came[0].size * len(came), bytes_accessed=12 * came[0].size, transcendentals=0
        ),
        compiler_params=pltpu.CompilerParams(vmem_limit_bytes=2 * MIB),
        name="add_shares",
    )(info, *on_chip((part, *came)))


def score_kernel(info, *refs):
    out = refs[-1]
    for half in range(2):
        own, left, right = refs[3 * half : 3 * half + 3]
        for j in range(left.shape[0]):
            total = own[j] + left[j] + right[j]
            width = total.shape[-1] // 2
            product = total[:, :width] * total[:, width:]
            sources = width // 16
            ranked = product.T.reshape(2 * sources, 8, product.shape[0])
            summed = jnp.sum(ranked, axis=1)
            line = jnp.concatenate([summed[:sources], summed[sources:]], axis=1)
            for n in range(sources):
                out[info[3 + n], 2 * half + j, :] = line[n]


def score(info, terms):
    seqs, tokens, _ = terms[0].shape
    return pl.pallas_call(
        score_kernel,
        in_specs=[SMEM] + [VMEM] * 6,
        out_specs=VMEM,
        out_shape=jax.ShapeDtypeStruct((16, 2 * seqs, 2 * tokens), jnp.float32),
        compiler_params=pltpu.CompilerParams(vmem_limit_bytes=4 * MIB),
        name="score",
    )(info, *on_chip(terms))


def choose_kernel(where, returned, out, rows):
    queries, count, tokens = out.shape
    lines = returned.shape[0]
    rows[:lines] = returned[:, :tokens]
    rows[lines:] = returned[:, tokens:]
    for q in range(queries):
        for c in range(count):
            out[q, c, :] = rows[where[HEAD + q * count + c]]


def choose(where, returned, queries, count):
    lines, width = returned.shape
    return pl.pallas_call(
        choose_kernel,
        in_specs=[SMEM, VMEM],
        out_specs=VMEM,
        out_shape=jax.ShapeDtypeStruct((queries, count, width // 2), jnp.float32),
        scratch_shapes=[pltpu.VMEM((2 * lines, width // 2), jnp.float32)],
        compiler_params=pltpu.CompilerParams(vmem_limit_bytes=4 * MIB),
        name="choose",
    )(where, *on_chip([returned]))


def local(candidates, sequence_place, activations, gradients, query_in, query_out):
    queries, count = candidates.shape
    total = sequence_place.shape[0]
    shares = lax.axis_size("tensor")
    device = lax.axis_index("dp")
    z = lax.axis_index("tensor")
    core = device % 2
    chip = device // 2

    other_acts = lax.ppermute(activations, "dp", PARTNER)
    other_grads = lax.ppermute(gradients, "dp", PARTNER)

    positions = jnp.arange(total, dtype=jnp.int32)
    target_rows = jnp.sum(
        jnp.where(candidates[:, :, None] == positions, sequence_place, 0), axis=2
    )
    listed = jnp.any(target_rows[:, :, None] == positions, axis=1)
    number = jnp.arange(queries, dtype=jnp.int32)[:, None]
    flags = listed.astype(jnp.int32)
    before = jnp.sum(
        jnp.where(number[:, :, None] > number[None, :, 0:1].reshape(1, queries, 1), flags[None], 0),
        axis=1,
    )
    slot_query = jnp.stack(
        [jnp.sum(jnp.where(listed & (before == m), number, 0), axis=0) for m in range(2)]
    )
    table = slot_query.reshape(1, 1, 2 * total).astype(jnp.bfloat16)
    block = jnp.concatenate(
        [query_in, query_out, jnp.broadcast_to(table, (queries, 8, 2 * total))], axis=-1
    )

    def dp(array, phase, distance):
        return lax.ppermute(array, "dp", hop(phase, distance))

    blocks = []
    lines = [("block", block), ("below", dp(block, 1, 1))]
    lines += [("above", dp(block, 1, -1)), ("far", dp(block, 1, 2))]
    for name, array in lines:
        up, down = dp(array, 2, 1), dp(array, 2, -1)
        on = dp(up, 2, 1) if name == "below" else dp(down, 2, -1)
        blocks += [array, up, down, on]

    offsets = jnp.array(OFFSETS, jnp.int32)
    y, x = chip // SIDE, chip % SIDE
    second_axis, first_axis = offsets[:, 0], offsets[:, 1]
    row = (y + jnp.where(core == 0, second_axis, first_axis)) % SIDE
    col = (x + jnp.where(core == 0, first_axis, second_axis)) % SIDE
    slot = jnp.sum(jnp.where(target_rows[:, :, None] == positions, before[:, None, :], 0), axis=2)
    kind = jnp.where((target_rows // 2) % 2 == core, 0, 2) + target_rows % 2
    where = slot * total + (target_rows // 4) * 4 + kind
    heads = jnp.stack([z, 2 * device, 2 * (device ^ 1)])
    info = jnp.concatenate([heads, row * SIDE + col, where.reshape(-1)]).astype(jnp.int32)

    ring = {1: [(i, (i + 1) % shares) for i in range(shares)]}
    ring[-1] = [(i, (i - 1) % shares) for i in range(shares)]

    def send(array, sign):
        return lax.ppermute(array, "tensor", ring[sign])

    (one,) = hold(info, (activations, 0))
    two, held_grads = hold(info, (activations, 1), (gradients, None))
    other_one, other_two = hold(info, (other_acts, 0), (other_acts, 1))
    held_a = ((one, two), held_grads)
    held_b = ((other_one, other_two), other_grads)
    far_a, far_b = shares // 2, shares - 1 - shares // 2
    streams = []
    for base, held, lengths in ((1, held_a, (far_a, far_b)), (2, held_b, (far_b, far_a))):
        part, own, plus, minus = project(info, base, blocks, *held, shares, lengths)
        streams.append([own, send(plus, 1), send(minus, -1), part, lengths])
    for step in range(1, far_a):
        for stream in streams:
            _, plus, minus, part, lengths = stream
            came, signs = [], []
            for sign, array, length in ((1, plus, lengths[0]), (-1, minus, lengths[1])):
                if step < length:
                    came.append(array)
                    signs.append(sign)
            away = [s * (lengths[0 if s > 0 else 1] - step) for s in signs]
            sums = add_shares(info, part, came, away)
            for sign, total_so_far in zip(signs, sums):
                stream[1 if sign > 0 else 2] = send(total_so_far, sign)

    scores = score(info, [a for stream in streams for a in stream[:3]])
    returned = lax.all_to_all(
        scores, "dp", split_axis=0, concat_axis=0, tiled=True, axis_index_groups=SAME_CORE
    )

    return choose(info, returned.reshape(64, -1), queries, count)


def solution(mesh):
    return jax.shard_map(
        local,
        mesh=mesh,
        in_specs=(
            P("dp", None),
            P(),
            P("dp", None, "tensor"),
            P("dp", None, "tensor"),
            P("dp", None, "tensor"),
            P("dp", None, "tensor"),
        ),
        out_specs=P("dp", None, "tensor"),
        check_vma=False,
    )
```
